256 devices in a mesh: occ: 256 (over x, y, z, core).
Axes of the slice: x: 4, y: 4, z: 8, core: 2. Of those that a mesh axis runs over, the one named last changes fastest.
Arguments:
- ri_factors: bfloat16 [256, 512, 1536], P('occ'), may hold values from -1.09375 to 1.09375
- occ_energy: float32 [256], P('occ'), may hold values from -1.5 to -0.3
- vir_energy: float32 [512], replicated, may hold values from 0.2 to 2.5
- partner: int32 [2, 256], P(None, 'occ'), may hold values from 0 to 255, as said below
- pair_weight: int32 [2, 256], P(None, 'occ'), may hold values from 1 to 2, as said below
Outputs:
- response: float32 [256, 512, 1536], P('occ')
- aux_density: float32 [1536, 1536], P('occ')
The draws below stay inside these ranges and needn't reach their ends.
Inputs may be any that keep to these rules, and one draw needn't show every extreme that they name: In each round the partner of orbital i is i XOR m for one nonzero m of that round, so partners pair up and the pair list is symmetric; in the first round m = 128. `pair_weight`: the two orbitals of a pair carry the same weight in a round.
All inputs are finite; a program needn't handle non-finite values.
Results may differ from the reference program's by a relative error of at most 0.0036.
Values may be sent and summed in bfloat16 or wider, within the bound.
No kernel may reach another device: no remote copies, remote signals or barrier semaphores. Data moves between devices by JAX's collectives and lax.ppermute only.
A program may use at most 64 MiB of HBM per device.

```python
import jax
import jax.numpy as jnp
from jax import lax

V = 512
NAUX = 1536
ROUNDS = 2
NOCC = 256


def round_masks(key):
    later = jax.random.randint(jax.random.fold_in(key, 11), (ROUNDS - 1,), 1, NOCC).astype(jnp.int32)
    first = jnp.full((1,), NOCC // 2, jnp.int32)
    return jnp.concatenate([first, later]).astype(jnp.int32)


def draw_partner(key, part):
    masks = round_masks(key)
    orbitals = jnp.arange(NOCC, dtype=jnp.int32)
    return jnp.bitwise_xor(orbitals[None, :], masks[:, None]).astype(jnp.int32)


def draw_pair_weight(key, part):
    masks = round_masks(key)
    orbitals = jnp.arange(NOCC, dtype=jnp.int32)
    partners = jnp.bitwise_xor(orbitals[None, :], masks[:, None]).astype(jnp.int32)
    lowest = jnp.minimum(orbitals[None, :], partners)
    coins = jax.random.randint(jax.random.fold_in(key, 23), (ROUNDS, NOCC), 0, 2)
    weights = 1 + jnp.take_along_axis(coins, lowest, axis=1)
    rounds_col = jnp.arange(ROUNDS, dtype=jnp.int32)[:, None]
    weights = jnp.where((rounds_col == 0) & (lowest == 0), 2, weights)
    weights = jnp.where((rounds_col == 1) & (lowest == 0), 1, weights)
    return weights.astype(jnp.int32)


def block_scale(key, extent, cuts, least, top_value):
    loudness, own = 1.0, jax.random.fold_in(key, 6)
    for position, shards_of in cuts:
        draws = jnp.exp(jax.random.uniform(jax.random.fold_in(own, position), (shards_of,), jnp.float32, least / len(cuts), top_value / len(cuts)))
        loudness = loudness * jnp.repeat(draws, extent[position] // shards_of).reshape([-1 if axis == position else 1 for axis in range(len(extent))])
    return loudness


def centred(key, dims, deviation, most, pieces=(), kind=jnp.bfloat16):
    array = jax.random.normal(key, dims, jnp.float32) * deviation
    if len(pieces) > 0:
        array = block_scale(key, dims, pieces, -0.22, 0.18) * array
    return jnp.clip(array, min=-most, max=most).astype(kind)


def setup_inputs(seed: int = 0) -> dict:
    arg_keys = jax.random.split(jax.random.key(seed), 6)
    return {
        "ri_factors": centred(arg_keys[0], (NOCC, V, NAUX), 0.18, 1.09375, ((0, 256),)),
        "occ_energy": jnp.clip(-1.5 + 1.2 * jax.random.uniform(arg_keys[1], (NOCC,), jnp.float32) ** block_scale(arg_keys[1], (NOCC,), ((0, 256),), -0.2, 0.2), -1.5, -0.3),
        "vir_energy": jnp.clip(jax.random.uniform(arg_keys[2], (V,), jnp.float32, 0.2, 2.5), 0.2, 2.5),
        "partner": draw_partner(jax.random.fold_in(arg_keys[5], 71), 0),
        "pair_weight": draw_pair_weight(jax.random.fold_in(arg_keys[5], 71), 0),
    }


def reference(ri_factors, occ_energy, vir_energy, partner, pair_weight):
    def orbital(density, orbital_idx):
        own_block = ri_factors[orbital_idx]
        accumulated = jnp.zeros((V, NAUX), jnp.float32)
        for round_num in range(ROUNDS):
            other = partner[round_num, orbital_idx].astype(jnp.int32)
            fetched = lax.dynamic_index_in_dim(ri_factors, other, 0, keepdims=False)
            coulomb = jnp.dot(own_block, fetched.T, preferred_element_type=jnp.float32)
            denominator = occ_energy[orbital_idx] + occ_energy[other] - vir_energy[:, None] - vir_energy[None, :]
            amplitudes = coulomb / denominator
            combined = (2.0 * amplitudes - amplitudes.T).astype(jnp.bfloat16)
            weight_now = pair_weight[round_num, orbital_idx].astype(jnp.float32)
            response_part = (weight_now * jnp.dot(combined, fetched, preferred_element_type=jnp.float32)).astype(jnp.bfloat16)
            accumulated = accumulated + response_part.astype(jnp.float32)
            density = density + jnp.dot(response_part.T, own_block, preferred_element_type=jnp.float32)
        return density, accumulated

    density, responses = lax.scan(orbital, jnp.zeros((NAUX, NAUX), jnp.float32), jnp.arange(NOCC, dtype=jnp.int32))
    return responses, density / NOCC
```

```python
import jax
import jax.numpy as jnp
from jax import lax
from jax.sharding import PartitionSpec as P

ROUNDS = 2
NX, NY, NZ, NC = 4, 4, 8, 2
DEVICES = NX * NY * NZ * NC
FIRST_MASK = DEVICES // 2
PAD_ROWS = 16


def coords(device):
    return device >> 6 & 3, device >> 4 & 3, device >> 1 & 7, device & 1


def index_of(x, y, z, core):
    return ((x * NY + y) * NZ + z) * NC + core


def swap(value, mask):
    return lax.ppermute(value, "occ", [(s, s ^ mask) for s in range(DEVICES)])


def row_owner(x, y, z, core):
    return ((core * NX + x) * NY + y) * NZ + z


def to_owner(value, step):
    pairs = []
    for s in range(DEVICES):
        x, y, z, core = coords(s)
        pairs.append((s, row_owner(x, y, z ^ step, core)))
    return lax.ppermute(value, "occ", pairs)


def energy_rows(energy, width):
    high = lax.reduce_precision(energy, 8, 7)
    rest = energy - high
    middle = lax.reduce_precision(rest, 8, 7)
    low = rest - middle
    lane = lax.broadcasted_iota(jnp.int32, (PAD_ROWS, width), 1)
    rows = jnp.where(lane == 0, high, jnp.where(lane == 1, middle, jnp.where(lane == 2, low, 0.0)))
    return rows.astype(jnp.bfloat16)


def energy_of(packed, count):
    pieces = packed[count, :3].astype(jnp.float32)
    return pieces[0] + pieces[1] + pieces[2]


def part_of(own, fetched, own_energy, other_energy, vir_energy, weight):
    coulomb = lax.dot_general(own, fetched, (((1,), (1,)), ((), ())), preferred_element_type=jnp.float32)
    denominator = own_energy + other_energy - vir_energy[:, None] - vir_energy[None, :]
    amplitudes = coulomb / denominator
    combined = (2.0 * amplitudes - amplitudes.T).astype(jnp.bfloat16)
    product = jnp.dot(combined, fetched, preferred_element_type=jnp.float32)
    return (weight * product).astype(jnp.bfloat16)


def pieces_first(block, me):
    return [lax.dynamic_index_in_dim(block, jnp.bitwise_xor(me, step), 0, keepdims=False) for step in range(block.shape[0])]


def reduce_over(block, me, bit):
    total = None
    for step, piece in enumerate(pieces_first(block, me)):
        if step == 0:
            total = piece
        else:
            total = total + swap(piece.astype(jnp.bfloat16), step << bit).astype(jnp.float32)
    return total


def body(ri_factors, occ_energy, vir_energy, partner, pair_weight):
    own = ri_factors[0]
    count, width = own.shape
    half = width // 2
    me = lax.axis_index("occ")
    x, y, z, core = coords(me)
    own_energy = occ_energy[0]

    fetched0 = swap(own, FIRST_MASK)
    energy0 = swap(occ_energy, FIRST_MASK)[0]

    packed = jnp.concatenate([own, energy_rows(own_energy, width)], 0)
    packed_core = swap(packed, 1)
    own_core = packed_core[:count]

    mask = jnp.bitwise_xor(partner[1, 0], me)
    sending = jnp.where(jnp.bitwise_and(mask, 1) == 1, packed_core, packed)
    branches = [lambda block: block]
    for chip_mask in range(1, DEVICES // 2):
        branches.append(lambda block, m=2 * chip_mask: swap(block, m))
    packed1 = lax.switch(jnp.right_shift(mask, 1), branches, sending)
    fetched1 = packed1[:count]
    energy1 = energy_of(packed1, count)

    weights = pair_weight[:, 0].astype(jnp.float32)
    parts = [
        part_of(own, fetched0, own_energy, energy0, vir_energy, weights[0]),
        part_of(own, fetched1, own_energy, energy1, vir_energy, weights[1]),
    ]
    response = parts[0].astype(jnp.float32) + parts[1].astype(jnp.float32)

    rows = jnp.zeros((half, width), jnp.float32)
    upper = core == 1
    for part in parts:
        low, high = part[:, :half], part[:, half:]
        keep = jnp.where(upper, high, low)
        give = jnp.where(upper, low, high)
        got = swap(give, 1)
        for lhs, rhs in ((keep, own), (got, own_core)):
            rows = rows + lax.dot_general(lhs, rhs, (((0,), (0,)), ((), ())), preferred_element_type=jnp.float32)

    deep, fine = half // NX, half // (NX * NY)
    left = rows[:, :half].reshape(NX, deep, half)
    right = rows[:, half:].reshape(NX, NY, fine, half).transpose(1, 0, 2, 3)
    left = reduce_over(left, x, 6).reshape(NY, fine, half)
    right = reduce_over(right, y, 4)
    left = reduce_over(left, y, 4)
    right = reduce_over(right, x, 6)
    mine = jnp.concatenate([left, right], 1).reshape(NZ, fine // NZ, width)
    density = None
    for step, piece in enumerate(pieces_first(mine, z)):
        arrived = to_owner(piece, step)
        density = arrived if density is None else density + arrived
    return response[None], density / float(DEVICES)


def solution(mesh):
    placed = (P("occ", None, None), P("occ"), P(), P(None, "occ"), P(None, "occ"))
    return jax.shard_map(
        body,
        mesh=mesh,
        in_specs=placed,
        out_specs=(P("occ", None, None), P("occ", None)),
        check_vma=False,
    )
```

```python
import jax
import jax.numpy as jnp
from jax import lax
from jax.sharding import PartitionSpec as P

ROUNDS = 2
NX, NY, NZ, NC = 4, 4, 8, 2
DEVICES = NX * NY * NZ * NC
FIRST_MASK = DEVICES // 2
PAD_ROWS = 16


def coords(device):
    return device >> 6 & 3, device >> 4 & 3, device >> 1 & 7, device & 1


def swap(value, mask):
    return lax.ppermute(value, "occ", [(s, s ^ mask) for s in range(DEVICES)])


def groups(key):
    members = {}
    for device in range(DEVICES):
        members.setdefault(key(*coords(device)), []).append(device)
    return list(members.values())


PLANES = groups(lambda x, y, z, core: (z, core))
COLUMNS = groups(lambda x, y, z, core: (x, y))


def exchange(value, members):
    return lax.all_to_all(value, "occ", 0, 0, axis_index_groups=members, tiled=True)


def swap_by(mask, block):
    z_mask, y_mask, x_mask = mask & 7, mask >> 3 & 3, mask >> 5 & 3

    def over_z(high):
        leaves = [
            (lambda value, m=high * NZ + low: swap(value, 2 * m) if m else value) for low in range(NZ)
        ]
        return lambda value: lax.switch(z_mask, leaves, value)

    def over_y(high):
        return lambda value: lax.switch(y_mask, [over_z(high * NY + low) for low in range(NY)], value)

    return lax.switch(x_mask, [over_y(high) for high in range(NX)], block)


def energy_rows(energy, width):
    high = lax.reduce_precision(energy, 8, 7)
    rest = energy - high
    middle = lax.reduce_precision(rest, 8, 7)
    low = rest - middle
    lane = lax.broadcasted_iota(jnp.int32, (PAD_ROWS, width), 1)
    rows = jnp.where(lane == 0, high, jnp.where(lane == 1, middle, jnp.where(lane == 2, low, 0.0)))
    return rows.astype(jnp.bfloat16)


def energy_of(packed, count):
    pieces = packed[count, :3].astype(jnp.float32)
    return pieces[0] + pieces[1] + pieces[2]


def part_of(own, fetched, own_energy, other_energy, vir_energy, weight):
    coulomb = lax.dot_general(own, fetched, (((1,), (1,)), ((), ())), preferred_element_type=jnp.float32)
    denominator = own_energy + other_energy - vir_energy[:, None] - vir_energy[None, :]
    amplitudes = coulomb / denominator
    combined = (2.0 * amplitudes - amplitudes.T).astype(jnp.bfloat16)
    product = jnp.dot(combined, fetched, preferred_element_type=jnp.float32)
    return (weight * product).astype(jnp.bfloat16)


def body(ri_factors, occ_energy, vir_energy, partner, pair_weight):
    own = ri_factors[0]
    count, width = own.shape
    half = width // 2
    me = lax.axis_index("occ")
    core = me & 1

    own_core, energy_core = swap(own, 1), swap(occ_energy, 1)
    fetched0, energy0 = swap(own, FIRST_MASK), swap(occ_energy, FIRST_MASK)

    mask = jnp.bitwise_xor(partner[1, 0], me)
    across = mask & 1 == 1
    sending = jnp.concatenate(
        [
            jnp.where(across, own_core, own),
            energy_rows(jnp.where(across, energy_core, occ_energy)[0], width),
        ],
        0,
    )
    packed1 = swap_by(jnp.right_shift(mask, 1), sending)
    packed1, fetched0 = lax.optimization_barrier((packed1, fetched0))
    fetched1 = packed1[:count]
    energy1 = energy_of(packed1, count)

    weights = pair_weight[:, 0].astype(jnp.float32)
    parts = [
        part_of(own, fetched0, occ_energy[0], energy0[0], vir_energy, weights[0]),
        part_of(own, fetched1, occ_energy[0], energy1, vir_energy, weights[1]),
    ]
    response = parts[0].astype(jnp.float32) + parts[1].astype(jnp.float32)

    def my_columns(block):
        return jnp.where(core == 1, block[:, half:], block[:, :half])

    density = jnp.zeros((width, half), jnp.float32)
    for part in parts:
        for lhs, rhs in ((part, own), (swap(part, 1), own_core)):
            density = density + lax.dot_general(
                lhs, my_columns(rhs), (((0,), (0,)), ((), ())), preferred_element_type=jnp.float32
            )

    chips = NX * NY
    pieces = exchange(density.astype(jnp.bfloat16).reshape(chips, width // chips, half), PLANES)
    pieces = jnp.sum(pieces.astype(jnp.float32), 0)
    last = NZ * NC
    pieces = exchange(pieces.reshape(last, width // (chips * last), half), COLUMNS)
    pieces = jnp.sum(pieces.reshape(NZ, NC, width // (chips * last), half), 0)
    rows = jnp.concatenate([pieces[0], pieces[1]], 1)
    return response[None], rows / float(DEVICES)


def solution(mesh):
    placed = (P("occ", None, None), P("occ"), P(), P(None, "occ"), P(None, "occ"))
    return jax.shard_map(
        body,
        mesh=mesh,
        in_specs=placed,
        out_specs=(P("occ", None, None), P("occ", None)),
        check_vma=False,
    )
```

```python
import jax
import jax.numpy as jnp
from jax import lax
from jax.experimental import pallas as pl
from jax.experimental.pallas import tpu as pltpu
from jax.sharding import PartitionSpec as P

ROUNDS = 2
NX, NY, NZ, NC = 4, 4, 8, 2
DEVICES = NX * NY * NZ * NC
FIRST_MASK = DEVICES // 2
LANES = 128


def coords(device):
    return device >> 6 & 3, device >> 4 & 3, device >> 1 & 7, device & 1


def swap(value, mask):
    return lax.ppermute(value, "occ", [(s, s ^ mask) for s in range(DEVICES)])


def groups(key):
    members = {}
    for device in range(DEVICES):
        members.setdefault(key(*coords(device)), []).append(device)
    return list(members.values())


PLANES = groups(lambda x, y, z, core: (z, core))
EVERYONE = groups(lambda x, y, z, core: 0)
COLUMNS = groups(lambda x, y, z, core: (x, y))


def exchange(value, members):
    return lax.all_to_all(value, "occ", 0, 0, axis_index_groups=members, tiled=True)


def energy_columns(energy, rows):
    high = lax.reduce_precision(energy, 8, 7)
    rest = energy - high
    middle = lax.reduce_precision(rest, 8, 7)
    low = rest - middle
    lane = lax.broadcasted_iota(jnp.int32, (rows, LANES), 1)
    columns = jnp.where(lane == 0, high, jnp.where(lane == 1, middle, jnp.where(lane == 2, low, 0.0)))
    return columns.astype(jnp.bfloat16)


def reorder_kernel(mask_ref, source_ref, target_ref):
    mask = mask_ref[0] & (DEVICES - 1)
    width = target_ref.shape[2]

    def step(index, carry):
        target_ref[index] = source_ref[jnp.bitwise_xor(index, mask), :, :width]
        return carry

    lax.fori_loop(0, DEVICES, step, 0, unroll=8)


def reorder(mask, spread, width):
    return pl.pallas_call(
        reorder_kernel,
        out_shape=jax.ShapeDtypeStruct(spread.shape[:2] + (width,), spread.dtype),
        in_specs=[pl.BlockSpec(memory_space=pltpu.SMEM), pl.BlockSpec(memory_space=pltpu.VMEM)],
        out_specs=pl.BlockSpec(memory_space=pltpu.VMEM),
    )(mask[None], spread)


def part_of(own, fetched, own_energy, other_energy, vir_energy, weight):
    coulomb = lax.dot_general(own, fetched, (((1,), (1,)), ((), ())), preferred_element_type=jnp.float32)
    denominator = own_energy + other_energy - vir_energy[:, None] - vir_energy[None, :]
    amplitudes = coulomb / denominator
    combined = (2.0 * amplitudes - amplitudes.T).astype(jnp.bfloat16)
    product = jnp.dot(combined, fetched, preferred_element_type=jnp.float32)
    return (weight * product).astype(jnp.bfloat16)


def body(ri_factors, occ_energy, vir_energy, partner, pair_weight):
    own = ri_factors[0]
    count, width = own.shape
    half = width // 2
    me = lax.axis_index("occ")
    core = me & 1

    fetched0, energy0 = swap(own, FIRST_MASK), swap(occ_energy, FIRST_MASK)
    own_core = swap(own, 1)

    mask = jnp.bitwise_xor(partner[1, 0], me)
    run = count // DEVICES
    packed = jnp.concatenate([own, energy_columns(occ_energy[0], count)], 1)
    spread = exchange(packed.reshape(DEVICES, run, width + LANES), EVERYONE)
    pieces = jnp.sum(spread[:, 0, width : width + 3].astype(jnp.float32), 1)
    energy1 = jnp.sum(jnp.where(lax.iota(jnp.int32, DEVICES) == partner[1, 0], pieces, 0.0))
    fetched1 = exchange(reorder(mask, spread, width), EVERYONE).reshape(count, width)

    weights = pair_weight[:, 0].astype(jnp.float32)
    parts = [
        part_of(own, fetched0, occ_energy[0], energy0[0], vir_energy, weights[0]),
        part_of(own, fetched1, occ_energy[0], energy1, vir_energy, weights[1]),
    ]
    response = parts[0].astype(jnp.float32) + parts[1].astype(jnp.float32)

    def my_columns(block):
        return jnp.where(core == 1, block[:, half:], block[:, :half])

    density = jnp.zeros((width, half), jnp.float32)
    for part in parts:
        for lhs, rhs in ((part, own), (swap(part, 1), own_core)):
            density = density + lax.dot_general(
                lhs, my_columns(rhs), (((0,), (0,)), ((), ())), preferred_element_type=jnp.float32
            )

    chips = NX * NY
    pieces = exchange(density.astype(jnp.bfloat16).reshape(chips, width // chips, half), PLANES)
    pieces = jnp.sum(pieces.astype(jnp.float32), 0)
    last = NZ * NC
    pieces = exchange(pieces.reshape(last, width // (chips * last), half), COLUMNS)
    pieces = jnp.sum(pieces.reshape(NZ, NC, width // (chips * last), half), 0)
    rows = jnp.concatenate([pieces[0], pieces[1]], 1)
    return response[None], rows / float(DEVICES)


def solution(mesh):
    placed = (P("occ", None, None), P("occ"), P(), P(None, "occ"), P(None, "occ"))
    return jax.shard_map(
        body,
        mesh=mesh,
        in_specs=placed,
        out_specs=(P("occ", None, None), P("occ", None)),
        check_vma=False,
    )
```

```python
import jax
import jax.numpy as jnp
from jax import lax
from jax.experimental import pallas as pl
from jax.experimental.pallas import tpu as pltpu
from jax.sharding import PartitionSpec as P

ROUNDS = 2
NX, NY, NZ, NC = 4, 4, 8, 2
DEVICES = NX * NY * NZ * NC
FIRST_MASK = DEVICES // 2
LANES = 128
TILE = 128
DENSITY_TILE = 256


def coords(device):
    return device >> 6 & 3, device >> 4 & 3, device >> 1 & 7, device & 1


def swap(value, mask):
    return lax.ppermute(value, "occ", [(s, s ^ mask) for s in range(DEVICES)])


def groups(key):
    members = {}
    for device in range(DEVICES):
        members.setdefault(key(*coords(device)), []).append(device)
    return list(members.values())


PLANES = groups(lambda x, y, z, core: (z, core))
EVERYONE = groups(lambda x, y, z, core: 0)
COLUMNS = groups(lambda x, y, z, core: (x, y))


def exchange(value, members):
    return lax.all_to_all(value, "occ", 0, 0, axis_index_groups=members, tiled=True)


def energy_columns(energy, rows):
    high = lax.reduce_precision(energy, 8, 7)
    rest = energy - high
    middle = lax.reduce_precision(rest, 8, 7)
    low = rest - middle
    lane = lax.broadcasted_iota(jnp.int32, (rows, LANES), 1)
    columns = jnp.where(lane == 0, high, jnp.where(lane == 1, middle, jnp.where(lane == 2, low, 0.0)))
    return columns.astype(jnp.bfloat16)


def reorder_kernel(mask_ref, source_ref, target_ref):
    mask = mask_ref[0] & (DEVICES - 1)
    width = target_ref.shape[2]

    def step(index, carry):
        target_ref[index] = source_ref[jnp.bitwise_xor(index, mask), :, :width]
        return carry

    lax.fori_loop(0, DEVICES, step, 0, unroll=8)


def reorder(mask, spread, width):
    return pl.pallas_call(
        reorder_kernel,
        out_shape=jax.ShapeDtypeStruct(spread.shape[:2] + (width,), spread.dtype),
        in_specs=[pl.BlockSpec(memory_space=pltpu.SMEM), pl.BlockSpec(memory_space=pltpu.VMEM)],
        out_specs=pl.BlockSpec(memory_space=pltpu.VMEM),
    )(mask[None], spread)


def part_kernel(energy_ref, weight_ref, row_ref, column_ref, own_ref, fetched_ref, part_ref, amplitude_ref, combined_ref):
    energy, weight = energy_ref[0], weight_ref[0]
    count = own_ref.shape[0]

    @pl.loop(0, count // TILE)
    def _(step):
        rows = pl.ds(pl.multiple_of(step * TILE, TILE), TILE)
        coulomb = lax.dot_general(
            own_ref[rows, :], fetched_ref[...], (((1,), (1,)), ((), ())), preferred_element_type=jnp.float32
        )
        amplitude_ref[rows, :] = coulomb / (energy - column_ref[rows, :] - row_ref[...])

    for first in range(0, count, TILE):
        rows = slice(first, first + TILE)
        combined_ref[rows, :] = (2.0 * amplitude_ref[rows, :] - amplitude_ref[:, rows].T).astype(jnp.bfloat16)

    @pl.loop(0, count // TILE)
    def _(step):
        rows = pl.ds(pl.multiple_of(step * TILE, TILE), TILE)
        product = jnp.dot(combined_ref[rows, :], fetched_ref[...], preferred_element_type=jnp.float32)
        part_ref[rows, :] = (weight * product).astype(jnp.bfloat16)


def part_of(own, fetched, energy, vir_energy, weight):
    count = own.shape[0]
    whole = pl.BlockSpec(memory_space=pltpu.VMEM)
    scalar = pl.BlockSpec(memory_space=pltpu.SMEM)
    return pl.pallas_call(
        part_kernel,
        out_shape=jax.ShapeDtypeStruct(own.shape, jnp.bfloat16),
        in_specs=[scalar, scalar, whole, whole, whole, whole],
        out_specs=whole,
        scratch_shapes=[pltpu.VMEM((count, count), jnp.float32), pltpu.VMEM((count, count), jnp.bfloat16)],
        cost_estimate=pl.CostEstimate(
            flops=4 * count * count * own.shape[1], bytes_accessed=6 * own.size, transcendentals=0
        ),
    )(energy[None], weight[None], vir_energy[None, :], vir_energy[:, None], own, fetched)


def density_kernel(core_ref, first_ref, second_ref, far_first_ref, far_second_ref, own_ref, far_ref, out_ref):
    width = own_ref.shape[1]
    half = width // 2
    columns = pl.ds(pl.multiple_of(core_ref[0] * half, half), half)

    @pl.loop(0, width // DENSITY_TILE)
    def _(step):
        rows = pl.ds(pl.multiple_of(step * DENSITY_TILE, DENSITY_TILE), DENSITY_TILE)
        total = jnp.zeros((DENSITY_TILE, half), jnp.float32)
        for lhs_ref, rhs_ref in (
            (first_ref, own_ref),
            (second_ref, own_ref),
            (far_first_ref, far_ref),
            (far_second_ref, far_ref),
        ):
            total = total + lax.dot_general(
                lhs_ref[:, rows], rhs_ref[:, columns], (((0,), (0,)), ((), ())), preferred_element_type=jnp.float32
            )
        out_ref[rows, :] = total.astype(jnp.bfloat16)


def density_of(core, first, second, far_first, far_second, own, far):
    count, width = own.shape
    whole = pl.BlockSpec(memory_space=pltpu.VMEM)
    return pl.pallas_call(
        density_kernel,
        out_shape=jax.ShapeDtypeStruct((width, width // 2), jnp.bfloat16),
        in_specs=[pl.BlockSpec(memory_space=pltpu.SMEM)] + [whole] * 6,
        out_specs=whole,
        cost_estimate=pl.CostEstimate(
            flops=4 * count * width * width, bytes_accessed=14 * own.size, transcendentals=0
        ),
    )(core[None], first, second, far_first, far_second, own, far)


def body(ri_factors, occ_energy, vir_energy, partner, pair_weight):
    own = ri_factors[0]
    count, width = own.shape
    half = width // 2
    me = lax.axis_index("occ")
    core = me & 1

    fetched0 = swap(own, FIRST_MASK)
    own_core = swap(own, 1)

    mask = jnp.bitwise_xor(partner[1, 0], me)
    run = count // DEVICES
    packed = jnp.concatenate([own, energy_columns(occ_energy[0], count)], 1)
    spread = exchange(packed.reshape(DEVICES, run, width + LANES), EVERYONE)
    spread, fetched0, own_core = lax.optimization_barrier((spread, fetched0, own_core))
    pieces = jnp.sum(spread[:, 0, width : width + 3].astype(jnp.float32), 1)

    def pair_energy(other):
        return occ_energy[0] + jnp.sum(jnp.where(lax.iota(jnp.int32, DEVICES) == other, pieces, 0.0))

    fetched1 = exchange(reorder(mask, spread, width), EVERYONE).reshape(count, width)

    weights = pair_weight[:, 0].astype(jnp.float32)
    part0 = part_of(own, fetched0, pair_energy(partner[0, 0]), vir_energy, weights[0])
    far0 = swap(part0, 1)
    part1 = part_of(own, fetched1, pair_energy(partner[1, 0]), vir_energy, weights[1])
    far1 = swap(part1, 1)
    response = part0.astype(jnp.float32) + part1.astype(jnp.float32)
    density = density_of(core, part0, part1, far0, far1, own, own_core)

    chips = NX * NY
    pieces = exchange(density.reshape(chips, width // chips, half), PLANES)
    pieces = jnp.sum(pieces.astype(jnp.float32), 0)
    last = NZ * NC
    pieces = exchange(pieces.astype(jnp.bfloat16).reshape(last, width // (chips * last), half), COLUMNS)
    pieces = jnp.sum(pieces.reshape(NZ, NC, width // (chips * last), half).astype(jnp.float32), 0)
    rows = jnp.concatenate([pieces[0], pieces[1]], 1)
    return response[None], rows / float(DEVICES)


def solution(mesh):
    placed = (P("occ", None, None), P("occ"), P(), P(None, "occ"), P(None, "occ"))
    return jax.shard_map(
        body,
        mesh=mesh,
        in_specs=placed,
        out_specs=(P("occ", None, None), P("occ", None)),
        check_vma=False,
    )
```

```python
import jax
import jax.numpy as jnp
from jax import lax
from jax.experimental import pallas as pl
from jax.experimental.pallas import tpu as pltpu
from jax.sharding import PartitionSpec as P

NX, NY, NZ, NC = 4, 4, 8, 2
DEVICES = NX * NY * NZ * NC
FIRST_MASK = DEVICES // 2
LANES = 128
TILE = 128
SUBLANES = 8
GRANT = 20 << 20
DENSITY_TILE = 256


def coords(device):
    return device >> 6 & 3, device >> 4 & 3, device >> 1 & 7, device & 1


def swap(value, mask):
    return lax.ppermute(value, "occ", [(s, s ^ mask) for s in range(DEVICES)])


def groups(key):
    members = {}
    for device in range(DEVICES):
        members.setdefault(key(*coords(device)), []).append(device)
    return list(members.values())


PLANES = groups(lambda x, y, z, core: (z, core))
EVERYONE = groups(lambda x, y, z, core: 0)
COLUMNS = groups(lambda x, y, z, core: (x, y))


def exchange(value, members):
    return lax.all_to_all(value, "occ", 0, 0, axis_index_groups=members, tiled=True)


def pack_kernel(energy_ref, block_ref, packed_ref):
    count, width = block_ref.shape
    run = packed_ref.shape[1]
    lane = lax.broadcasted_iota(jnp.int32, (run, LANES), 1)
    rest = jnp.full((run, LANES), energy_ref[0], jnp.float32)
    columns = jnp.zeros((run, LANES), jnp.float32)
    for position in range(3):
        piece = rest.astype(jnp.bfloat16).astype(jnp.float32)
        columns = jnp.where(lane == position, piece, columns)
        rest = rest - piece
    columns = columns.astype(jnp.bfloat16)

    def step(index, carry):
        rows = block_ref[pl.ds(pl.multiple_of(index * SUBLANES, SUBLANES), SUBLANES), :]
        for part in range(SUBLANES // run):
            target = index * (SUBLANES // run) + part
            packed_ref[target, :, :width] = rows[part * run : (part + 1) * run]
            packed_ref[target, :, width:] = columns
        return carry

    lax.fori_loop(0, count // SUBLANES, step, 0, unroll=2)


def pack(energy, block):
    count, width = block.shape
    return pl.pallas_call(
        pack_kernel,
        out_shape=jax.ShapeDtypeStruct((DEVICES, count // DEVICES, width + LANES), block.dtype),
        in_specs=[pl.BlockSpec(memory_space=pltpu.SMEM), pl.BlockSpec(memory_space=pltpu.VMEM)],
        out_specs=pl.BlockSpec(memory_space=pltpu.VMEM),
        compiler_params=pltpu.CompilerParams(vmem_limit_bytes=GRANT),
    )(energy, block)


def reorder_kernel(mask_ref, source_ref, target_ref):
    mask = mask_ref[0] & (DEVICES - 1)
    width = target_ref.shape[2]

    def step(index, carry):
        target_ref[index] = source_ref[jnp.bitwise_xor(index, mask), :, :width]
        return carry

    lax.fori_loop(0, DEVICES, step, 0, unroll=8)


def reorder(mask, spread, width):
    return pl.pallas_call(
        reorder_kernel,
        out_shape=jax.ShapeDtypeStruct(spread.shape[:2] + (width,), spread.dtype),
        in_specs=[pl.BlockSpec(memory_space=pltpu.SMEM), pl.BlockSpec(memory_space=pltpu.VMEM)],
        out_specs=pl.BlockSpec(memory_space=pltpu.VMEM),
        compiler_params=pltpu.CompilerParams(vmem_limit_bytes=GRANT),
    )(mask[None], spread)


def part_kernel(energy_ref, weight_ref, row_ref, column_ref, own_ref, fetched_ref, part_ref, amplitude_ref, combined_ref):
    energy, weight = energy_ref[0], weight_ref[0]
    count = own_ref.shape[0]

    @pl.loop(0, count // TILE)
    def _(step):
        rows = pl.ds(pl.multiple_of(step * TILE, TILE), TILE)
        coulomb = lax.dot_general(
            own_ref[rows, :], fetched_ref[...], (((1,), (1,)), ((), ())), preferred_element_type=jnp.float32
        )
        amplitude_ref[rows, :] = coulomb / (energy - column_ref[rows, :] - row_ref[...])

    for first in range(0, count, TILE):
        rows = slice(first, first + TILE)
        combined_ref[rows, :] = (2.0 * amplitude_ref[rows, :] - amplitude_ref[:, rows].T).astype(jnp.bfloat16)

    @pl.loop(0, count // TILE)
    def _(step):
        rows = pl.ds(pl.multiple_of(step * TILE, TILE), TILE)
        product = jnp.dot(combined_ref[rows, :], fetched_ref[...], preferred_element_type=jnp.float32)
        part_ref[rows, :] = (weight * product).astype(jnp.bfloat16)


def part_of(own, fetched, energy, vir_energy, weight):
    count = own.shape[0]
    whole = pl.BlockSpec(memory_space=pltpu.VMEM)
    scalar = pl.BlockSpec(memory_space=pltpu.SMEM)
    return pl.pallas_call(
        part_kernel,
        out_shape=jax.ShapeDtypeStruct(own.shape, jnp.bfloat16),
        in_specs=[scalar, scalar, whole, whole, whole, whole],
        out_specs=whole,
        scratch_shapes=[pltpu.VMEM((count, count), jnp.float32), pltpu.VMEM((count, count), jnp.bfloat16)],
        compiler_params=pltpu.CompilerParams(vmem_limit_bytes=GRANT),
        cost_estimate=pl.CostEstimate(
            flops=4 * count * count * own.shape[1], bytes_accessed=6 * own.size, transcendentals=0
        ),
    )(energy[None], weight[None], vir_energy[None, :], vir_energy[:, None], own, fetched)


def density_kernel(core_ref, *refs):
    *pairs, out_ref = refs
    total = jnp.zeros(out_ref.shape, jnp.float32)
    if len(pairs) % 2:
        total = pairs.pop()[...]
    for lhs_ref, rhs_ref in zip(pairs[0::2], pairs[1::2]):
        total = total + lax.dot_general(
            lhs_ref[...], rhs_ref[...], (((0,), (0,)), ((), ())), preferred_element_type=jnp.float32
        )
    out_ref[...] = total.astype(out_ref.dtype)


def density_of(core, pairs, before, dtype):
    count, width = pairs[0][0].shape
    half = width // 2
    lhs = pl.BlockSpec((count, DENSITY_TILE), lambda step, core: (0, step))
    rhs = pl.BlockSpec((count, half), lambda step, core: (0, core[0]))
    tile = pl.BlockSpec((DENSITY_TILE, half), lambda step, core: (step, 0))
    operands = [operand for pair in pairs for operand in pair]
    specs = [lhs, rhs] * len(pairs)
    if before is not None:
        operands.append(before)
        specs.append(tile)
    return pl.pallas_call(
        density_kernel,
        out_shape=jax.ShapeDtypeStruct((width, half), dtype),
        grid_spec=pltpu.PrefetchScalarGridSpec(
            num_scalar_prefetch=1, grid=(width // DENSITY_TILE,), in_specs=specs, out_specs=tile
        ),
        compiler_params=pltpu.CompilerParams(vmem_limit_bytes=GRANT),
        cost_estimate=pl.CostEstimate(
            flops=2 * count * width * half * len(pairs), bytes_accessed=width * half * 8, transcendentals=0
        ),
    )(core[None], *operands)


def window(ri_factors, occ_energy, vir_energy, partner, pair_weight):
    own = ri_factors[0]
    count, width = own.shape
    half = width // 2
    me = lax.axis_index("occ")
    core = me & 1

    fetched0 = swap(own, FIRST_MASK)
    own_core = swap(own, 1)

    mask = jnp.bitwise_xor(partner[1, 0], me)
    packed = pack(occ_energy, own)
    spread = exchange(packed, EVERYONE)
    spread, own_core = lax.optimization_barrier((spread, own_core))
    pieces = jnp.sum(spread[:, 0, width : width + 3].astype(jnp.float32), 1)

    def pair_energy(other):
        return occ_energy[0] + jnp.sum(jnp.where(lax.iota(jnp.int32, DEVICES) == other, pieces, 0.0))

    ordered = reorder(mask, spread, width)
    fetched1 = exchange(ordered, EVERYONE).reshape(count, width)

    weights = pair_weight[:, 0].astype(jnp.float32)
    part0 = part_of(own, fetched0, pair_energy(partner[0, 0]), vir_energy, weights[0])
    far0 = swap(part0, 1)
    density = density_of(core, ((part0, own), (far0, own_core)), None, jnp.float32)
    part1 = part_of(own, fetched1, pair_energy(partner[1, 0]), vir_energy, weights[1])
    far1 = swap(part1, 1)
    density = density_of(core, ((part1, own),), density, jnp.float32)
    response = part0.astype(jnp.float32) + part1.astype(jnp.float32)
    density = density_of(core, ((far1, own_core),), density, jnp.bfloat16)

    chips = NX * NY
    pieces = exchange(density.reshape(chips, width // chips, half), PLANES)
    pieces = jnp.sum(pieces.astype(jnp.float32), 0)
    last = NZ * NC
    pieces = exchange(pieces.astype(jnp.bfloat16).reshape(last, width // (chips * last), half), COLUMNS)
    pieces = jnp.sum(pieces.reshape(NZ, NC, width // (chips * last), half).astype(jnp.float32), 0)
    rows = jnp.concatenate([pieces[0], pieces[1]], 1)
    return response[None], rows / float(DEVICES)


def solution(mesh):
    placed = (P("occ", None, None), P("occ"), P(), P(None, "occ"), P(None, "occ"))
    return jax.shard_map(
        window,
        mesh=mesh,
        in_specs=placed,
        out_specs=(P("occ", None, None), P("occ", None)),
        check_vma=False,
    )
```
